32 devices in a mesh: dp: 8 (over z, core), expert: 4 (over y, x).
Axes of the slice: x: 2, y: 2, z: 4, core: 2. Of those that a mesh axis runs over, the one named last changes fastest.
Arguments:
- tokens: bfloat16 [5120, 2048], P(('dp', 'expert')), may hold values from -6 to 6
- expert_ids: int32 [5120, 8], P(('dp', 'expert')), may hold values from 0 to 122, as said below
- gate_probs: float32 [5120, 8], P(('dp', 'expert')), may hold values from 0.02 to 1
- upstream: bfloat16 [5120, 2048], P(('dp', 'expert')), may hold values from -6 to 6
- w_gate: bfloat16 [4, 2048, 768], P('expert'), may hold values from -0.125 to 0.125
- w_up: bfloat16 [4, 2048, 768], P('expert'), may hold values from -0.125 to 0.125
- w_down: bfloat16 [4, 2048, 768], P('expert'), may hold values from -0.21875 to 0.21875
Outputs:
- layer_out: bfloat16 [5120, 2048], P(('dp', 'expert'))
- grad_tokens: bfloat16 [5120, 2048], P(('dp', 'expert'))
- grad_probs: float32 [5120, 8], P(('dp', 'expert'))
- grad_gate: float32 [4, 2048, 768], P('expert', 'dp')
- grad_up: float32 [4, 2048, 768], P('expert', 'dp')
- grad_down: float32 [4, 2048, 768], P('expert', 'dp')
The draws below stay inside these ranges and needn't reach their ends.
Inputs may be any that keep to these rules, and one draw needn't show every extreme that they name: `expert_ids`: slot 0 of every token names one of the experts 0 to 3, the experts computed here; slot k, for k from 1 to 7, names an expert from 4 + (k - 1) * 17 to 4 + k * 17 - 1. `expert_ids`: among the 160 tokens of one device, slot 0 names no expert more than 100 times; on every index of dp one expert is named by slot 0 exactly 100 times by the tokens of each device of that index.
All inputs are finite; a program needn't handle non-finite values.
Results may differ from the reference program's by a relative error of at most 0.0058.
Values may be sent and summed in bfloat16 or wider, within the bound.
A program may use at most 128 MiB of HBM per device.

```python
import math
import jax
import jax.numpy as jnp
from jax import lax

D = 2048
FF = 768
TOP = 8
TOK_DEV = 160
EXPERTS = 4
CAP = 100
GROUP = 17
TOKENS = 5120
N_DP = 8


def draw_expert_ids(key, part):
    blocks = TOKENS // TOK_DEV

    def one_block(block_index):
        row_key = jax.random.fold_in(jax.random.fold_in(key, 101), block_index // EXPERTS)
        hot_expert = jax.random.randint(row_key, (), 0, EXPERTS)
        block_key = jax.random.fold_in(jax.random.fold_in(key, 202), block_index)
        key_shuffle, key_jitter, key_others, key_later = jax.random.split(block_key, 4)
        shuffle = jax.random.permutation(key_shuffle, TOK_DEV)
        rank_in = jnp.argsort(shuffle).astype(jnp.int32)
        jitter = jax.random.randint(key_jitter, (TOK_DEV,), 0, 2)
        others = jax.random.permutation(key_others, EXPERTS - 1)
        other_slot = jnp.mod(rank_in - CAP + jitter, EXPERTS - 1)
        other_expert = jnp.mod(hot_expert + 1 + others[other_slot], EXPERTS)
        leading = jnp.where(rank_in < CAP, hot_expert, other_expert)
        later_slots = EXPERTS + jnp.arange(TOP - 1)[None, :] * GROUP + jax.random.randint(key_later, (TOK_DEV, TOP - 1), 0, GROUP)
        return jnp.concatenate([leading[:, None], later_slots], axis=1).astype(jnp.int32)
    return jax.vmap(one_block)(jnp.arange(blocks)).reshape(TOKENS, TOP).astype(jnp.int32)


def strengthened(drawn, own_key, source, target, shards_of, factor):
    def block_of(position):
        return (jnp.arange(drawn.shape[position]) // (drawn.shape[position] // shards_of)).reshape((-1,) + (1,) * (drawn.ndim - 1 - position))

    near = jax.random.permutation(own_key, shards_of)[block_of(target)]
    second = (block_of(target) + shards_of // 2) % shards_of
    return jnp.where((block_of(source) == near) | (block_of(source) == second), factor * drawn, drawn)


def shard_levels(own_key, dims, pieces, low, top_value):
    factor_of = 1.0
    for dim, parts in pieces:
        draws = jax.random.uniform(jax.random.fold_in(jax.random.fold_in(own_key, 6), dim), (parts,), jnp.float32, low / len(pieces), top_value / len(pieces))
        factor_of = factor_of * jnp.repeat(jnp.exp(draws), dims[dim] // parts).reshape((-1,) + (1,) * (len(dims) - 1 - dim))
    return factor_of


def normal_values(own_key, shape, deviation, limit, shards=(), kind=jnp.bfloat16):
    values = deviation * jax.random.normal(own_key, shape, jnp.float32)
    if shards:
        values = values * shard_levels(own_key, shape, shards, -0.22, 0.18)
    return jnp.clip(values, -limit, limit).astype(kind)


def noise_with(own_key, dims, deviation, limit, cuts, heavy, held_as=jnp.bfloat16):
    result = deviation * jax.random.normal(own_key, dims, jnp.float32)
    if cuts:
        result = result * shard_levels(own_key, dims, cuts, -0.22, 0.18)
    return jnp.clip(strengthened(result, jax.random.fold_in(own_key, 3), *heavy), -limit, limit).astype(held_as)


def setup_inputs(seed: int = 0) -> dict:
    key_of = jax.random.split(jax.random.key(seed), 8)
    tokens = noise_with(key_of[0], (TOKENS, D), 1.0, 6.0, ((0, 32),), (0, 1, 32, 2.75))
    expert_ids = draw_expert_ids(jax.random.fold_in(key_of[7], 71), 0)
    gate_probs = jnp.clip(jnp.exp(math.log(1.0) - 3.912023 * jax.random.uniform(key_of[2], (TOKENS, TOP), jnp.float32) ** shard_levels(key_of[2], (TOKENS, TOP), ((0, 32),), -0.2, 0.2)), 0.02, 1.0)
    upstream = normal_values(key_of[3], (TOKENS, D), 1.0, 6.0, ((0, 32),))
    w_gate = normal_values(key_of[4], (EXPERTS, D, FF), D ** -0.5, 0.125, ((0, 4),))
    w_up = normal_values(key_of[5], (EXPERTS, D, FF), D ** -0.5, 0.125, ((0, 4),))
    w_down = normal_values(key_of[6], (EXPERTS, D, FF), FF ** -0.5, 0.21875, ((0, 4),))
    return {"tokens": tokens, "expert_ids": expert_ids, "gate_probs": gate_probs, "upstream": upstream, "w_gate": w_gate, "w_up": w_up, "w_down": w_down}


def times_transposed(left, right):
    return lax.dot_general(left, right, (((1,), (1,)), ((), ())), preferred_element_type=jnp.float32)


def contract_rows(left, right):
    return lax.dot_general(left, right, (((0,), (0,)), ((), ())), preferred_element_type=jnp.float32)


def expert_pass(arrived, cot_rows, gate_mat, up_mat, down_mat):
    pre_gate = jnp.dot(arrived, gate_mat, preferred_element_type=jnp.float32)
    pre_up = jnp.dot(arrived, up_mat, preferred_element_type=jnp.float32)
    hidden = (pre_gate * jax.nn.sigmoid(pre_gate) * pre_up).astype(jnp.bfloat16)
    expert_out = times_transposed(hidden, down_mat).astype(jnp.bfloat16)
    grad_hidden = jnp.dot(cot_rows, down_mat, preferred_element_type=jnp.float32)
    sigmoid_gate = jax.nn.sigmoid(pre_gate)
    grad_pre_gate = (grad_hidden * pre_up * sigmoid_gate * (1.0 + pre_gate * (1.0 - sigmoid_gate))).astype(jnp.bfloat16)
    grad_pre_up = (grad_hidden * pre_gate * sigmoid_gate).astype(jnp.bfloat16)
    input_grad = (times_transposed(grad_pre_gate, gate_mat) + times_transposed(grad_pre_up, up_mat)).astype(jnp.bfloat16)
    return (expert_out, input_grad, contract_rows(arrived, grad_pre_gate),
            contract_rows(arrived, grad_pre_up), contract_rows(cot_rows, hidden))


def reference(tokens, expert_ids, gate_probs, upstream, w_gate, w_up, w_down):
    first_expert = expert_ids[:, 0].astype(jnp.int32)
    prob_total = jnp.sum(gate_probs, axis=1)
    gate_share = gate_probs[:, 0] / prob_total
    cotangent = (gate_share[:, None] * upstream.astype(jnp.float32)).astype(jnp.bfloat16)
    most_rows = N_DP * EXPERTS * CAP
    sorted_order = jnp.argsort(first_expert, stable=True).astype(jnp.int32)
    counts = jnp.sum((first_expert[:, None] == jnp.arange(EXPERTS, dtype=jnp.int32)[None, :]).astype(jnp.int32), axis=0)
    starts = (jnp.cumsum(counts) - counts).astype(jnp.int32)
    padded = jnp.concatenate([sorted_order, jnp.zeros((most_rows,), jnp.int32)])

    def one_expert(expert_index):
        row_index = lax.dynamic_slice(padded, (starts[expert_index],), (most_rows,))
        is_live = jnp.arange(most_rows, dtype=jnp.int32) < counts[expert_index]
        arrived = jnp.where(is_live[:, None], tokens[row_index], jnp.zeros((), tokens.dtype))
        cot_rows = jnp.where(is_live[:, None], cotangent[row_index], jnp.zeros((), cotangent.dtype))
        return expert_pass(arrived, cot_rows, w_gate[expert_index], w_up[expert_index], w_down[expert_index])

    outs_all, grads_all, grad_gate, grad_up, grad_down = lax.map(one_expert, jnp.arange(EXPERTS, dtype=jnp.int32))
    inverse = jnp.argsort(sorted_order).astype(jnp.int32)
    rank_in = (inverse - starts[first_expert]).astype(jnp.int32)
    mixed = outs_all[first_expert, rank_in]
    layer_out = (gate_share[:, None] * mixed.astype(jnp.float32)).astype(jnp.bfloat16)
    gate_product = jnp.sum(upstream.astype(jnp.float32) * mixed.astype(jnp.float32), axis=1)
    first_slot = (jnp.arange(TOP) == 0).astype(jnp.float32)
    grad_probs = (first_slot[None, :] - gate_share[:, None]) * (gate_product / prob_total)[:, None]
    grad_tokens = grads_all[first_expert, rank_in]
    return layer_out, grad_tokens, grad_probs, grad_gate, grad_up, grad_down
```

```python
import functools

import jax
import jax.numpy as jnp
from jax import lax
from jax.experimental import pallas as pl
from jax.experimental.pallas import tpu as pltpu
from jax.sharding import PartitionSpec as P

MESH = pl.DeviceIdType.MESH
F32 = jnp.float32
BF16 = jnp.bfloat16


def dot_nn(a, b):
    return lax.dot_general(a, b, (((1,), (0,)), ((), ())), preferred_element_type=F32)


def dot_nt(a, b):
    return lax.dot_general(a, b, (((1,), (1,)), ((), ())), preferred_element_type=F32)


def dot_tn(a, b):
    return lax.dot_general(a, b, (((0,), (0,)), ((), ())), preferred_element_type=F32)


def loop(count, body):
    def step(i, carry):
        body(i)
        return carry

    lax.fori_loop(0, count, step, 0)


def moe_kernel(
    owners, copies, cap,
    ids_ref, probs_ref, tok_ref, ups_ref, wg_hbm, wu_hbm, wd_hbm,
    out_ref, gtok_ref, gprob_ref, ggate_ref, gup_ref, gdown_ref,
    wg, wu, wd, onehot, xs, cs, xr, cr, ors, grs, pre_g, pre_u, hid, gpg, gpu,
    sib_s, sib_r, z_s, z_l, z_r, tmp,
    w_sem, x_ss, x_rs, c_ss, c_rs, o_ss, o_rs, g_ss, g_rs,
    sib_ss, sib_rs, z_ss, z_ls, z_rs,
):
    me = lax.axis_index("expert")
    dp = lax.axis_index("dp")
    levels = copies // 2
    core = lax.rem(dp, 2)
    z = dp // 2
    tok_count, width = tok_ref.shape
    ff = hid.shape[1]
    rows = width // copies
    ft = 256
    dt = 256
    sibling = {"dp": dp + 1 - 2 * core}
    right = {"dp": lax.rem(dp + 2, copies)}
    left = {"dp": lax.rem(dp + copies - 2, copies)}

    w_copies = [
        pltpu.make_async_copy(src.at[0], dst, w_sem.at[i])
        for i, (src, dst) in enumerate(((wg_hbm, wg), (wu_hbm, wu), (wd_hbm, wd)))
    ]
    for copy in w_copies:
        copy.start()

    barrier = pltpu.get_barrier_semaphore()

    def greet(k):
        pl.semaphore_signal(
            barrier, inc=1, device_id={"expert": lax.rem(me + k + 1, owners)}, device_id_type=MESH
        )

    loop(owners - 1, greet)
    pl.semaphore_signal(barrier, inc=1, device_id=sibling, device_id_type=MESH)

    @pl.when(z > 0)
    def _():
        pl.semaphore_signal(barrier, inc=1, device_id=left, device_id_type=MESH)

    @pl.when(z < levels - 1)
    def _():
        pl.semaphore_signal(barrier, inc=1, device_id=right, device_id_type=MESH)

    ids = ids_ref[...]
    experts = lax.broadcasted_iota(jnp.int32, (max(owners, 8), tok_count), 0)
    match = (experts == ids).astype(BF16)
    before = (
        lax.broadcasted_iota(jnp.int32, (tok_count, tok_count), 0)
        < lax.broadcasted_iota(jnp.int32, (tok_count, tok_count), 1)
    ).astype(BF16)
    rank = jnp.sum(dot_nn(match, before) * match.astype(F32), axis=0, keepdims=True)
    target = ids * cap + rank.astype(jnp.int32)
    slots = lax.broadcasted_iota(jnp.int32, (owners * cap, tok_count), 0)
    onehot[...] = (slots == target).astype(BF16)

    probs = probs_ref[...]
    total = jnp.sum(probs, axis=1, keepdims=True)
    share = probs[:, 0:1] / total

    def block(index):
        return pl.ds(pl.multiple_of(index * cap, 8), cap)

    def exchange(src, dst, ss, rs, k):
        peer = lax.rem(me + k + 1, owners)
        return pltpu.make_async_remote_copy(
            src_ref=src.at[block(peer)],
            dst_ref=dst.at[block(me)],
            send_sem=ss.at[k],
            recv_sem=rs.at[k],
            device_id={"expert": peer},
            device_id_type=MESH,
        )

    beside = (z + levels - 1) // levels + (2 * levels - 2 - z) // levels
    pl.semaphore_wait(barrier, owners + beside)

    def dispatch(values, src, dst, ss, rs):
        def one(k):
            peer = lax.rem(me + k + 1, owners)
            src[block(peer)] = dot_nn(onehot[block(peer)], values[...]).astype(BF16)
            exchange(src, dst, ss, rs, k).start()

        loop(owners - 1, one)
        dst[block(me)] = dot_nn(onehot[block(me)], values[...]).astype(BF16)

    dispatch(tok_ref, xs, xr, x_ss, x_rs)
    gtok_ref[...] = (share * ups_ref[...].astype(F32)).astype(BF16)
    dispatch(gtok_ref, cs, cr, c_ss, c_rs)

    w_copies[0].wait()
    w_copies[1].wait()
    loop(owners - 1, lambda k: exchange(xs, xr, x_ss, x_rs, k).wait_recv())

    def forward_tile(j):
        cols = pl.ds(pl.multiple_of(j * ft, 128), ft)
        a = dot_nn(xr[...], wg[:, cols])
        b = dot_nn(xr[...], wu[:, cols])
        pre_g[:, cols] = a
        pre_u[:, cols] = b
        hid[:, cols] = (a * jax.nn.sigmoid(a) * b).astype(BF16)

    loop(ff // ft, forward_tile)

    w_copies[2].wait()
    loop(owners - 1, lambda k: exchange(xs, xr, x_ss, x_rs, k).wait_send())

    def out_tile(j):
        cols = pl.ds(pl.multiple_of(j * dt, 128), dt)
        xs[:, cols] = dot_nt(hid[...], wd[cols, :]).astype(BF16)

    loop(width // dt, out_tile)
    ors[block(me)] = xs[block(me)]

    loop(owners - 1, lambda k: exchange(cs, cr, c_ss, c_rs, k).wait_recv())

    sides = ((cr, hid), (xr, gpg), (xr, gpu))

    def piece(m, dest):
        lhs, rhs = sides[m]
        cols = pl.ds(pl.multiple_of(dest * rows, 128), rows)
        return dot_tn(lhs[:, cols], rhs[...])

    def sib_copy(slot):
        return pltpu.make_async_remote_copy(
            src_ref=sib_s.at[slot], dst_ref=sib_r.at[slot],
            send_sem=sib_ss.at[slot], recv_sem=sib_rs.at[slot],
            device_id=sibling, device_id_type=MESH,
        )

    def right_copy(slot):
        return pltpu.make_async_remote_copy(
            src_ref=z_s.at[slot], dst_ref=z_l.at[slot],
            send_sem=z_ss.at[slot], recv_sem=z_ls.at[slot],
            device_id=right, device_id_type=MESH,
        )

    def left_copy(slot):
        return pltpu.make_async_remote_copy(
            src_ref=z_s.at[slot], dst_ref=z_r.at[slot],
            send_sem=z_ss.at[slot], recv_sem=z_rs.at[slot],
            device_id=left, device_id_type=MESH,
        )

    upper = z // (levels // 2)

    def to_sibling(m):
        def one(s):
            level = upper * s + (1 - upper) * (levels - 1 - s)
            slot = m * levels + level
            sib_s[slot] = piece(m, level * 2 + 1 - core).astype(BF16)
            sib_copy(slot).start()

        loop(levels, one)

    def chip_sum(m, level):
        slot = m * levels + level
        own = piece(m, level * 2 + core)
        sib_copy(slot).wait_recv()
        tmp[...] = own + sib_r[slot].astype(F32)

    def along_line(m):
        def one(s):
            far = levels - 1 - s

            @pl.when(far > z)
            def _():
                slot = m * levels + far
                chip_sum(m, far)

                @pl.when(z > 0)
                def _():
                    right_copy(slot).wait_recv()
                    tmp[...] += z_l[slot].astype(F32)

                z_s[slot] = tmp[...].astype(BF16)
                right_copy(slot).start()

            @pl.when(s < z)
            def _():
                slot = m * levels + s
                chip_sum(m, s)

                @pl.when(z < levels - 1)
                def _():
                    left_copy(slot).wait_recv()
                    tmp[...] += z_r[slot].astype(F32)

                z_s[slot] = tmp[...].astype(BF16)
                left_copy(slot).start()

        loop(levels - 1, one)

    def finish(m, dst):
        slot = m * levels + z
        chip_sum(m, z)

        @pl.when(z > 0)
        def _():
            right_copy(slot).wait_recv()
            tmp[...] += z_l[slot].astype(F32)

        @pl.when(z < levels - 1)
        def _():
            left_copy(slot).wait_recv()
            tmp[...] += z_r[slot].astype(F32)

        dst[0] = tmp[...]

    to_sibling(0)
    loop(owners - 1, lambda k: exchange(xs, ors, o_ss, o_rs, k).start())

    def backward_tile(j):
        cols = pl.ds(pl.multiple_of(j * ft, 128), ft)
        grad = dot_nn(cr[...], wd[:, cols])
        a = pre_g[:, cols]
        s = jax.nn.sigmoid(a)
        gpg[:, cols] = (grad * pre_u[:, cols] * s * (1.0 + a * (1.0 - s))).astype(BF16)
        gpu[:, cols] = (grad * a * s).astype(BF16)

    loop(ff // ft, backward_tile)
    to_sibling(1)
    to_sibling(2)
    along_line(0)

    loop(owners - 1, lambda k: exchange(cs, cr, c_ss, c_rs, k).wait_send())

    def grad_tile(j):
        cols = pl.ds(pl.multiple_of(j * dt, 128), dt)
        cs[:, cols] = (dot_nt(gpg[...], wg[cols, :]) + dot_nt(gpu[...], wu[cols, :])).astype(BF16)

    loop(width // dt, grad_tile)
    grs[block(me)] = cs[block(me)]
    loop(owners - 1, lambda k: exchange(cs, grs, g_ss, g_rs, k).start())

    along_line(1)
    along_line(2)

    loop(owners - 1, lambda k: exchange(xs, ors, o_ss, o_rs, k).wait_recv())
    product = jnp.zeros((tok_count, 1), F32)
    for j in range(width // dt):
        cols = pl.ds(j * dt, dt)
        mixed = dot_tn(onehot[...], ors[:, cols])
        out_ref[:, cols] = (share * mixed).astype(BF16)
        product += jnp.sum(ups_ref[:, cols].astype(F32) * mixed, axis=1, keepdims=True)
    first = (lax.broadcasted_iota(jnp.int32, probs.shape, 1) == 0).astype(F32)
    gprob_ref[...] = (first - share) * (product / total)

    loop(owners - 1, lambda k: exchange(cs, grs, g_ss, g_rs, k).wait_recv())

    def unpack_tile(j):
        cols = pl.ds(pl.multiple_of(j * dt, 128), dt)
        gtok_ref[:, cols] = dot_tn(onehot[...], grs[:, cols]).astype(BF16)

    loop(width // dt, unpack_tile)

    finish(0, gdown_ref)
    finish(1, ggate_ref)
    finish(2, gup_ref)

    loop(owners - 1, lambda k: exchange(xs, ors, o_ss, o_rs, k).wait_send())
    loop(owners - 1, lambda k: exchange(cs, grs, g_ss, g_rs, k).wait_send())
    loop(3 * levels, lambda slot: sib_copy(slot).wait_send())

    def sent(slot):
        @pl.when(lax.rem(slot, levels) != z)
        def _():
            right_copy(slot).wait_send()

    loop(3 * levels, sent)


def per_device(tokens, expert_ids, gate_probs, upstream, w_gate, w_up, w_down):
    tok_count, width = tokens.shape
    owners = lax.axis_size("expert")
    copies = lax.axis_size("dp")
    ff = w_gate.shape[2]
    capacity = tok_count // owners * 5 // 2
    cap = -(-capacity // CAP_ALIGN) * CAP_ALIGN
    slots = owners * cap
    levels = copies // 2
    rows = width // copies
    vmem = pl.BlockSpec(memory_space=pltpu.VMEM)
    hbm = pl.BlockSpec(memory_space=pl.ANY)
    dma = pltpu.SemaphoreType.DMA
    weight = pltpu.VMEM((width, ff), BF16)
    wide = pltpu.VMEM((slots, width), BF16)
    narrow = pltpu.VMEM((slots, ff), BF16)
    stack = pltpu.VMEM((3 * levels, rows, ff), BF16)
    grad = jax.ShapeDtypeStruct((1, rows, ff), F32)
    return pl.pallas_call(
        functools.partial(moe_kernel, owners, copies, cap),
        out_shape=(
            jax.ShapeDtypeStruct((tok_count, width), BF16),
            jax.ShapeDtypeStruct((tok_count, width), BF16),
            jax.ShapeDtypeStruct(gate_probs.shape, F32),
            grad, grad, grad,
        ),
        in_specs=[vmem, vmem, vmem, vmem, hbm, hbm, hbm],
        out_specs=(vmem,) * 6,
        scratch_shapes=[
            weight, weight, weight,
            pltpu.VMEM((slots, tok_count), BF16),
            wide, wide, wide, wide, wide, wide,
            pltpu.VMEM((slots, ff), F32), pltpu.VMEM((slots, ff), F32),
            narrow, narrow, narrow,
            stack, stack, stack, stack, stack,
            pltpu.VMEM((rows, ff), F32),
            dma((3,)),
            *[dma((owners - 1,))] * 8,
            *[dma((3 * levels,))] * 5,
        ],
        compiler_params=pltpu.CompilerParams(
            collective_id=0, has_side_effects=True, vmem_limit_bytes=62 * 2**20
        ),
    )(expert_ids[:, 0].reshape(1, -1), gate_probs, tokens, upstream, w_gate, w_up, w_down)


CAP_ALIGN = 16


def solution(mesh):
    rows = P(("dp", "expert"), None)
    experts = P("expert", None, None)
    grads = P("expert", "dp", None)
    return jax.shard_map(
        per_device,
        mesh=mesh,
        in_specs=(rows, rows, rows, rows, experts, experts, experts),
        out_specs=(rows, rows, rows, grads, grads, grads),
        check_vma=False,
    )
```

```python
import functools

import jax
import jax.numpy as jnp
from jax import lax
from jax.experimental import pallas as pl
from jax.experimental.pallas import tpu as pltpu
from jax.sharding import PartitionSpec as P

MESH = pl.DeviceIdType.MESH
F32 = jnp.float32
BF16 = jnp.bfloat16


def dot_nn(a, b):
    return lax.dot_general(a, b, (((1,), (0,)), ((), ())), preferred_element_type=F32)


def dot_nt(a, b):
    return lax.dot_general(a, b, (((1,), (1,)), ((), ())), preferred_element_type=F32)


def dot_tn(a, b):
    return lax.dot_general(a, b, (((0,), (0,)), ((), ())), preferred_element_type=F32)


def loop(count, body):
    def step(i, carry):
        body(i)
        return carry

    lax.fori_loop(0, count, step, 0)


def moe_kernel(
    owners, copies, cap,
    ids_ref, probs_ref, tok_ref, ups_ref, wg_hbm, wu_hbm, wd_hbm,
    out_ref, gtok_ref, gprob_ref, ggate_ref, gup_ref, gdown_ref,
    wg, wu, wd, onehot, xs, cs, xr, cr, ors, grs, pre_g, pre_u, hid, gpg, gpu,
    sib_s, sib_r, z_s, z_l, z_r, tmp,
    w_sem, x_ss, x_rs, c_ss, c_rs, o_ss, o_rs, g_ss, g_rs,
    sib_ss, sib_rs, z_ss, z_ls, z_rs,
):
    me = lax.axis_index("expert")
    dp = lax.axis_index("dp")
    levels = copies // 2
    core = lax.rem(dp, 2)
    z = dp // 2
    tok_count, width = tok_ref.shape
    ff = hid.shape[1]
    rows = width // copies
    ft = 256
    dt = 256
    sibling = {"dp": dp + 1 - 2 * core}
    right = {"dp": lax.rem(dp + 2, copies)}
    left = {"dp": lax.rem(dp + copies - 2, copies)}

    w_copies = [
        pltpu.make_async_copy(src.at[0], dst, w_sem.at[i])
        for i, (src, dst) in enumerate(((wg_hbm, wg), (wu_hbm, wu), (wd_hbm, wd)))
    ]
    for copy in w_copies:
        copy.start()

    barrier = pltpu.get_barrier_semaphore()

    def greet(k):
        pl.semaphore_signal(
            barrier, inc=1, device_id={"expert": lax.rem(me + k + 1, owners)}, device_id_type=MESH
        )

    loop(owners - 1, greet)
    pl.semaphore_signal(barrier, inc=1, device_id=sibling, device_id_type=MESH)

    @pl.when(z > 0)
    def _():
        pl.semaphore_signal(barrier, inc=1, device_id=left, device_id_type=MESH)

    @pl.when(z < levels - 1)
    def _():
        pl.semaphore_signal(barrier, inc=1, device_id=right, device_id_type=MESH)

    ids = ids_ref[0:1, :]
    experts = lax.broadcasted_iota(jnp.int32, (max(owners, 8), tok_count), 0)
    match = (experts == ids).astype(BF16)
    before = (
        lax.broadcasted_iota(jnp.int32, (tok_count, tok_count), 0)
        < lax.broadcasted_iota(jnp.int32, (tok_count, tok_count), 1)
    ).astype(BF16)
    rank = jnp.sum(dot_nn(match, before) * match.astype(F32), axis=0, keepdims=True)
    target = ids * cap + rank.astype(jnp.int32)
    slots = lax.broadcasted_iota(jnp.int32, (owners * cap, tok_count), 0)
    onehot[...] = (slots == target).astype(BF16)

    probs = probs_ref[...]
    total = jnp.sum(probs, axis=0, keepdims=True)
    share_row = probs[0:1, :] / total
    share = jnp.transpose(jnp.broadcast_to(share_row, (8, tok_count)))[:, 0:1]

    def block(index):
        return pl.ds(pl.multiple_of(index * cap, 8), cap)

    def exchange(src, dst, ss, rs, k):
        peer = lax.rem(me + k + 1, owners)
        return pltpu.make_async_remote_copy(
            src_ref=src.at[block(peer)],
            dst_ref=dst.at[block(me)],
            send_sem=ss.at[k],
            recv_sem=rs.at[k],
            device_id={"expert": peer},
            device_id_type=MESH,
        )

    beside = (z + levels - 1) // levels + (2 * levels - 2 - z) // levels
    pl.semaphore_wait(barrier, owners + beside)

    def dispatch(values, src, dst, ss, rs):
        def one(k):
            peer = lax.rem(me + k + 1, owners)
            src[block(peer)] = dot_nn(onehot[block(peer)], values[...]).astype(BF16)
            exchange(src, dst, ss, rs, k).start()

        loop(owners - 1, one)
        dst[block(me)] = dot_nn(onehot[block(me)], values[...]).astype(BF16)

    dispatch(tok_ref, xs, xr, x_ss, x_rs)
    gtok_ref[...] = (share * ups_ref[...].astype(F32)).astype(BF16)

    upper = z // (levels // 2)
    chunk = 2 * rows

    def level_at(s):
        return upper * s + (1 - upper) * (levels - 1 - s)

    def cot_copy(s, k):
        peer = lax.rem(me + k + 1, owners)
        cols = pl.ds(pl.multiple_of(level_at(s) * chunk, 128), chunk)
        index = s * (owners - 1) + k
        return pltpu.make_async_remote_copy(
            src_ref=cs.at[block(peer), cols],
            dst_ref=cr.at[block(me), cols],
            send_sem=c_ss.at[index],
            recv_sem=c_rs.at[index],
            device_id={"expert": peer},
            device_id_type=MESH,
        )

    def send_chunk(s):
        cols = pl.ds(pl.multiple_of(level_at(s) * chunk, 128), chunk)
        cs[:, cols] = dot_nn(onehot[...], gtok_ref[:, cols]).astype(BF16)
        loop(owners - 1, lambda k: cot_copy(s, k).start())
        cr[block(me), cols] = cs[block(me), cols]

    loop(levels, send_chunk)

    w_copies[0].wait()
    w_copies[1].wait()
    loop(owners - 1, lambda k: exchange(xs, xr, x_ss, x_rs, k).wait_recv())

    def forward_tile(j):
        cols = pl.ds(pl.multiple_of(j * ft, 128), ft)
        a = dot_nn(xr[...], wg[:, cols])
        b = dot_nn(xr[...], wu[:, cols])
        pre_g[:, cols] = a
        pre_u[:, cols] = b
        hid[:, cols] = (a * jax.nn.sigmoid(a) * b).astype(BF16)

    loop(ff // ft, forward_tile)

    sides = ((cr, hid), (xr, gpg), (xr, gpu))

    def piece(m, dest):
        lhs, rhs = sides[m]
        cols = pl.ds(pl.multiple_of(dest * rows, 128), rows)
        return dot_tn(lhs[:, cols], rhs[...])

    def sib_copy(slot):
        return pltpu.make_async_remote_copy(
            src_ref=sib_s.at[slot], dst_ref=sib_r.at[slot],
            send_sem=sib_ss.at[slot], recv_sem=sib_rs.at[slot],
            device_id=sibling, device_id_type=MESH,
        )

    def right_copy(slot):
        return pltpu.make_async_remote_copy(
            src_ref=z_s.at[slot], dst_ref=z_l.at[slot],
            send_sem=z_ss.at[slot], recv_sem=z_ls.at[slot],
            device_id=right, device_id_type=MESH,
        )

    def left_copy(slot):
        return pltpu.make_async_remote_copy(
            src_ref=z_s.at[slot], dst_ref=z_r.at[slot],
            send_sem=z_ss.at[slot], recv_sem=z_rs.at[slot],
            device_id=left, device_id_type=MESH,
        )

    def to_sibling(m, s):
        level = level_at(s)
        slot = m * levels + level
        sib_s[slot] = piece(m, level * 2 + 1 - core).astype(BF16)
        sib_copy(slot).start()

    def chip_sum(m, level):
        slot = m * levels + level
        own = piece(m, level * 2 + core)
        sib_copy(slot).wait_recv()
        tmp[...] = own + sib_r[slot].astype(F32)

    def along_line(m, s):
        far = levels - 1 - s

        @pl.when(far > z)
        def _():
            slot = m * levels + far
            chip_sum(m, far)

            @pl.when(z > 0)
            def _():
                right_copy(slot).wait_recv()
                tmp[...] += z_l[slot].astype(F32)

            z_s[slot] = tmp[...].astype(BF16)
            right_copy(slot).start()

        @pl.when(s < z)
        def _():
            slot = m * levels + s
            chip_sum(m, s)

            @pl.when(z < levels - 1)
            def _():
                left_copy(slot).wait_recv()
                tmp[...] += z_r[slot].astype(F32)

            z_s[slot] = tmp[...].astype(BF16)
            left_copy(slot).start()

    def finish(m, dst):
        slot = m * levels + z
        chip_sum(m, z)

        @pl.when(z > 0)
        def _():
            right_copy(slot).wait_recv()
            tmp[...] += z_l[slot].astype(F32)

        @pl.when(z < levels - 1)
        def _():
            left_copy(slot).wait_recv()
            tmp[...] += z_r[slot].astype(F32)

        dst[0] = tmp[...]

    edge = z * (levels - 1 - z) == 0

    def first_matrix(s):
        loop(owners - 1, lambda k: cot_copy(s, k).wait_recv())
        to_sibling(0, s)

        @pl.when(jnp.logical_and(edge, s > 0))
        def _():
            along_line(0, s - 1)

    loop(levels, first_matrix)

    w_copies[2].wait()

    def backward_tile(j):
        cols = pl.ds(pl.multiple_of(j * ft, 128), ft)
        grad = dot_nn(cr[...], wd[:, cols])
        a = pre_g[:, cols]
        s = jax.nn.sigmoid(a)
        gpg[:, cols] = (grad * pre_u[:, cols] * s * (1.0 + a * (1.0 - s))).astype(BF16)
        gpu[:, cols] = (grad * a * s).astype(BF16)

    loop(ff // ft, backward_tile)
    loop(levels, lambda s: to_sibling(1, s))
    loop(levels, lambda s: to_sibling(2, s))

    @pl.when(edge)
    def _():
        loop(levels - 1, lambda s: along_line(1, s))
        loop(levels - 1, lambda s: along_line(2, s))

    @pl.when(jnp.logical_not(edge))
    def _():
        loop(levels - 1, lambda s: along_line(0, s))

    loop(owners - 1, lambda k: exchange(xs, xr, x_ss, x_rs, k).wait_send())

    def out_tile(j):
        cols = pl.ds(pl.multiple_of(j * dt, 128), dt)
        xs[:, cols] = dot_nt(hid[...], wd[cols, :]).astype(BF16)

    loop(width // dt, out_tile)
    ors[block(me)] = xs[block(me)]
    loop(owners - 1, lambda k: exchange(xs, ors, o_ss, o_rs, k).start())

    loop(levels, lambda s: loop(owners - 1, lambda k: cot_copy(s, k).wait_send()))

    def grad_tile(j):
        cols = pl.ds(pl.multiple_of(j * dt, 128), dt)
        cs[:, cols] = (dot_nt(gpg[...], wg[cols, :]) + dot_nt(gpu[...], wu[cols, :])).astype(BF16)

    loop(width // dt, grad_tile)
    grs[block(me)] = cs[block(me)]
    loop(owners - 1, lambda k: exchange(cs, grs, g_ss, g_rs, k).start())

    @pl.when(jnp.logical_not(edge))
    def _():
        loop(levels - 1, lambda s: along_line(1, s))
        loop(levels - 1, lambda s: along_line(2, s))

    loop(owners - 1, lambda k: exchange(xs, ors, o_ss, o_rs, k).wait_recv())
    product = jnp.zeros((tok_count, 1), F32)
    for j in range(width // dt):
        cols = pl.ds(j * dt, dt)
        mixed = dot_tn(onehot[...], ors[:, cols])
        out_ref[:, cols] = (share * mixed).astype(BF16)
        product += jnp.sum(ups_ref[:, cols].astype(F32) * mixed, axis=1, keepdims=True)
    first = (lax.broadcasted_iota(jnp.int32, probs.shape, 0) == 0).astype(F32)
    product_row = jnp.transpose(jnp.broadcast_to(product, (tok_count, 128)))[0:1, :]
    gprob_ref[...] = (first - share_row) * (product_row / total)

    loop(owners - 1, lambda k: exchange(cs, grs, g_ss, g_rs, k).wait_recv())

    def unpack_tile(j):
        cols = pl.ds(pl.multiple_of(j * dt, 128), dt)
        gtok_ref[:, cols] = dot_tn(onehot[...], grs[:, cols]).astype(BF16)

    loop(width // dt, unpack_tile)

    finish(0, gdown_ref)
    finish(1, ggate_ref)
    finish(2, gup_ref)

    loop(owners - 1, lambda k: exchange(xs, ors, o_ss, o_rs, k).wait_send())
    loop(owners - 1, lambda k: exchange(cs, grs, g_ss, g_rs, k).wait_send())
    loop(3 * levels, lambda slot: sib_copy(slot).wait_send())

    def sent(slot):
        @pl.when(lax.rem(slot, levels) != z)
        def _():
            right_copy(slot).wait_send()

    loop(3 * levels, sent)


def per_device(tokens, expert_ids, gate_probs, upstream, w_gate, w_up, w_down):
    tok_count, width = tokens.shape
    owners = lax.axis_size("expert")
    copies = lax.axis_size("dp")
    ff = w_gate.shape[2]
    capacity = tok_count // owners * 5 // 2
    cap = -(-capacity // CAP_ALIGN) * CAP_ALIGN
    slots = owners * cap
    levels = copies // 2
    rows = width // copies
    vmem = pl.BlockSpec(memory_space=pltpu.VMEM)
    hbm = pl.BlockSpec(memory_space=pl.ANY)
    dma = pltpu.SemaphoreType.DMA
    weight = pltpu.VMEM((width, ff), BF16)
    wide = pltpu.VMEM((slots, width), BF16)
    narrow = pltpu.VMEM((slots, ff), BF16)
    stack = pltpu.VMEM((3 * levels, rows, ff), BF16)
    grad = jax.ShapeDtypeStruct((1, rows, ff), F32)
    layer_out, grad_tokens, grad_probs, grad_gate, grad_up, grad_down = pl.pallas_call(
        functools.partial(moe_kernel, owners, copies, cap),
        out_shape=(
            jax.ShapeDtypeStruct((tok_count, width), BF16),
            jax.ShapeDtypeStruct((tok_count, width), BF16),
            jax.ShapeDtypeStruct(gate_probs.shape[::-1], F32),
            grad, grad, grad,
        ),
        in_specs=[vmem, vmem, vmem, vmem, hbm, hbm, hbm],
        out_specs=(vmem,) * 6,
        scratch_shapes=[
            weight, weight, weight,
            pltpu.VMEM((slots, tok_count), BF16),
            wide, wide, wide, wide, wide, wide,
            pltpu.VMEM((slots, ff), F32), pltpu.VMEM((slots, ff), F32),
            narrow, narrow, narrow,
            stack, stack, stack, stack, stack,
            pltpu.VMEM((rows, ff), F32),
            dma((3,)),
            dma((owners - 1,)), dma((owners - 1,)),
            dma((levels * (owners - 1),)), dma((levels * (owners - 1),)),
            *[dma((owners - 1,))] * 4,
            *[dma((3 * levels,))] * 5,
        ],
        compiler_params=pltpu.CompilerParams(
            collective_id=0, has_side_effects=True, vmem_limit_bytes=62 * 2**20
        ),
    )(expert_ids.T, gate_probs.T, tokens, upstream, w_gate, w_up, w_down)
    return (layer_out, grad_tokens, grad_probs.T, grad_gate, grad_up, grad_down)


CAP_ALIGN = 16


def solution(mesh):
    rows = P(("dp", "expert"), None)
    experts = P("expert", None, None)
    grads = P("expert", "dp", None)
    return jax.shard_map(
        per_device,
        mesh=mesh,
        in_specs=(rows, rows, rows, rows, experts, experts, experts),
        out_specs=(rows, rows, rows, grads, grads, grads),
        check_vma=False,
    )
```
